32 devices in a mesh: freq: 4 (over z), space: 8 (over y, x, core).
Axes of the slice: x: 2, y: 2, z: 4, core: 2. Of those that a mesh axis runs over, the one named last changes fastest.
Arguments:
- recorded: bfloat16 [8, 2, 2048, 128], P('freq', None, 'space'), may hold values from -6 to 6
- v_factors: bfloat16 [8, 8, 2, 2048, 128], P('freq', None, None, 'space'), may hold values from -0.25 to 0.25
- u_factors: bfloat16 [8, 2, 2048, 8, 128], P('freq', None, 'space'), may hold values from -0.25 to 0.25
- tile_ranks: int32 [8, 8, 8], P('freq'), may hold values from 0 to 128, as said below
- mute_start: int32 [2048, 128], P('space', 'freq'), may hold values from 0 to 127
Outputs:
- muted_traces: float32 [2048, 128, 128], P('space', 'freq')
The draws below stay inside these ranges and needn't reach their ends.
Inputs may be any that keep to these rules, and one draw needn't show every extreme that they name: `tile_ranks`: entries with i equal to j are 128; every other entry is 0 or 64.
All inputs are finite; a program needn't handle non-finite values.
Results may differ from the reference program's by a relative error of at most 0.0041.
Values may be sent and summed in bfloat16 or wider, within the bound.
A program may use at most 64 MiB of HBM per device.

```python
import math
import jax
import jax.numpy as jnp
from jax import lax

TILE = 256
RMAX = 128
NS = 128
NT = 128
F = 8
NTILE = 8
NR = 2048


def draw_tile_ranks(key, part):
    tile_count = NR // TILE
    rolled_values = jax.random.randint(key, (F, tile_count, tile_count), 0, 9)
    levels = jnp.where(rolled_values < 4, RMAX // 2, 0)
    lines = jnp.arange(tile_count, dtype=jnp.int32)
    diagonal = (lines[:, None] == lines[None, :])[None, :, :]
    return jnp.where(diagonal, RMAX, levels).astype(jnp.int32)


def with_ends(entries, rng, smallest, largest):
    longest = entries.shape.index(max(entries.shape))
    spots = []
    for shift in (0, 1):
        where = [jax.random.randint(jax.random.fold_in(rng, axis), (), 0, length) for axis, length in enumerate(entries.shape)]
        where[longest] = (where[longest] + shift) % entries.shape[longest]
        spots.append(tuple(where))
    return entries.at[spots[0]].set(smallest).at[spots[1]].set(largest)


def shard_levels(own_key, shape, shards, low, top_value):
    loudness = 1.0
    for position, parts in shards:
        steps = jax.random.uniform(jax.random.fold_in(jax.random.fold_in(own_key, 6), position), (parts,), jnp.float32, low / len(shards), top_value / len(shards))
        loudness = loudness * jnp.repeat(jnp.exp(steps), shape[position] // parts).reshape((-1,) + (1,) * (len(shape) - 1 - position))
    return loudness


def gaussian(rng, dims, scale, limit, cuts=(), kind=jnp.bfloat16):
    drawn = jax.random.normal(rng, dims, jnp.float32) * scale
    if len(cuts) > 0:
        drawn = shard_levels(rng, dims, cuts, -0.22, 0.18) * drawn
    return jnp.clip(drawn, min=-limit, max=limit).astype(kind)


def setup_inputs(seed: int = 0) -> dict:
    key_list = jax.random.split(jax.random.key(seed), 6)
    return {
        "recorded": gaussian(key_list[0], (F, 2, NR, NS), 1.0, 6.0, ((0, 4), (2, 8))),
        "v_factors": gaussian(key_list[1], (F, NTILE, 2, NR, RMAX), (2 * TILE) ** -0.5, 0.25, ((0, 4), (3, 8))),
        "u_factors": gaussian(key_list[2], (F, 2, NR, NTILE, RMAX), (2 * (RMAX + (NTILE - 1) * RMAX * 2 // 9)) ** -0.5, 0.25, ((0, 4), (2, 8))),
        "tile_ranks": draw_tile_ranks(jax.random.fold_in(key_list[5], 71), 0),
        "mute_start": with_ends(jax.random.randint(key_list[4], (NR, NS), 0, NT), jax.random.fold_in(key_list[4], 1), 0, NT - 1).astype(jnp.int32),
    }


def reference(recorded, v_factors, u_factors, tile_ranks, mute_start):
    tile_count = NR // TILE
    spectra_list = []
    for slot in range(F):
        data_freq = recorded[slot].astype(jnp.float32).reshape(2, tile_count, TILE, NS)
        v_freq = v_factors[slot].reshape(tile_count, 2, tile_count, TILE, RMAX)
        u_freq = jnp.moveaxis(u_factors[slot].reshape(2, tile_count, TILE, tile_count, RMAX), 1, 0)

        def one_row(row_items):
            v_row, u_row, rank_row = row_items
            v_row = v_row.astype(jnp.float32)
            u_row = u_row.astype(jnp.float32)
            high = lax.Precision.HIGHEST
            block_real = jnp.einsum('jqk,jqs->jks', v_row[0], data_freq[0], precision=high) - jnp.einsum('jqk,jqs->jks', v_row[1], data_freq[1], precision=high)
            block_imag = jnp.einsum('jqk,jqs->jks', v_row[0], data_freq[1], precision=high) + jnp.einsum('jqk,jqs->jks', v_row[1], data_freq[0], precision=high)
            kept = (jnp.arange(RMAX, dtype=jnp.int32)[None, :] < rank_row[:, None])[:, :, None]
            block_real = lax.optimization_barrier(jnp.where(kept, block_real, 0.0).astype(jnp.bfloat16)).astype(jnp.float32)
            block_imag = lax.optimization_barrier(jnp.where(kept, block_imag, 0.0).astype(jnp.bfloat16)).astype(jnp.float32)
            real_part = jnp.einsum('pjk,jks->ps', u_row[0], block_real, precision=high) - jnp.einsum('pjk,jks->ps', u_row[1], block_imag, precision=high)
            imag_part = jnp.einsum('pjk,jks->ps', u_row[0], block_imag, precision=high) + jnp.einsum('pjk,jks->ps', u_row[1], block_real, precision=high)
            return jnp.stack([real_part, imag_part]).astype(jnp.bfloat16)
        row_spectra = lax.map(one_row, (v_freq, u_freq, tile_ranks[slot]))
        spectra_list.append(jnp.moveaxis(row_spectra, 1, 0).reshape(2, NR, NS))
    spectra = lax.optimization_barrier(jnp.stack(spectra_list)).astype(jnp.float32)
    freq_index = jnp.arange(F, dtype=jnp.int32)
    weights = 1 + freq_index * (NT // 2 // F)
    times = jnp.arange(NT, dtype=jnp.int32)
    phase = (weights[:, None] * times[None, :] % NT).astype(jnp.float32) * (2.0 * math.pi / NT)
    scale = 1.0 / math.sqrt(2.0 * F)
    cos_basis = jnp.cos(phase) * scale
    sin_basis = -jnp.sin(phase) * scale
    high = lax.Precision.HIGHEST
    traces = jnp.einsum('fps,ft->pst', spectra[:, 0], cos_basis, precision=high) + jnp.einsum('fps,ft->pst', spectra[:, 1], sin_basis, precision=high)
    return jnp.where(times[None, None, :] >= mute_start[:, :, None], traces, 0.0)
```

```python
import functools
import math

import jax
import jax.numpy as jnp
import ml_dtypes
import numpy as np
from jax import lax
from jax.experimental import pallas as pl
from jax.experimental.pallas import tpu as pltpu
from jax.sharding import PartitionSpec as P

NT = 128
GROUP = 8
NT_DIMS = (((1,), (1,)), ((), ()))


def flipped(index, mask):
    result = index
    bit = 1
    while bit <= mask:
        if mask & bit:
            result = result + bit * (1 - 2 * ((index // bit) % 2))
        bit *= 2
    return result


def send_order(count):
    return sorted(range(count), key=lambda r: (-bin(r >> 1).count("1"), r % 2, r))


def spectra_kernel(
    tiles, parts, ranks_ref, recorded_ref, v_hbm, u_hbm, out_ref,
    v_ref, u_ref, wide_ref, data_ref, send_ref, recv_ref, own_ref, factor_ref, spec_ref,
    v_sems, u_sems, send_sems, recv_sems, zsend_sems, zrecv_sems,
):
    me = lax.axis_index("space")
    me_z = lax.axis_index("freq")
    freqs = recorded_ref.shape[0]
    tile = recorded_ref.shape[2]
    sources = recorded_ref.shape[3]
    ranks = v_ref.shape[3]
    half = ranks // 2
    share = sources // parts
    order = send_order(tiles)

    v_copies = [
        pltpu.make_async_copy(v_hbm.at[f], v_ref.at[f], v_sems.at[f]) for f in range(freqs)
    ]
    u_copies = [
        pltpu.make_async_copy(u_hbm.at[f], u_ref.at[f], u_sems.at[f]) for f in range(freqs)
    ]
    for f in range(freqs):
        v_copies[f].start()
    for f in range(freqs):
        u_copies[f].start()

    barrier = pltpu.get_barrier_semaphore()
    for r in range(1, tiles):
        pl.semaphore_signal(
            barrier, inc=1, device_id={"space": flipped(me, r)}, device_id_type=pl.DeviceIdType.MESH
        )
    for r in range(1, parts):
        pl.semaphore_signal(
            barrier, inc=1, device_id={"freq": lax.rem(me_z + r, parts)},
            device_id_type=pl.DeviceIdType.MESH,
        )

    def space_copy(f, r):
        return pltpu.make_async_remote_copy(
            src_ref=send_ref.at[f, r],
            dst_ref=recv_ref.at[f, me],
            send_sem=send_sems.at[f, r],
            recv_sem=recv_sems.at[f, r],
            device_id={"space": flipped(me, r)},
            device_id_type=pl.DeviceIdType.MESH,
        )

    def freq_copy(f, r):
        target = lax.rem(me_z + r, parts)
        return pltpu.make_async_remote_copy(
            src_ref=spec_ref.at[f, pl.ds(pl.multiple_of(target * share, share), share)],
            dst_ref=out_ref.at[me_z, f],
            send_sem=zsend_sems.at[f, r],
            recv_sem=zrecv_sems.at[f, r],
            device_id={"freq": target},
            device_id_type=pl.DeviceIdType.MESH,
        )

    for f in range(freqs):
        real = recorded_ref[f, 0].astype(jnp.float32).T.astype(jnp.bfloat16)
        imag = recorded_ref[f, 1].astype(jnp.float32).T.astype(jnp.bfloat16)
        data_ref[f, :sources, :tile] = real
        data_ref[f, :sources, tile:] = -imag
        data_ref[f, sources:, :tile] = imag
        data_ref[f, sources:, tile:] = real

    lane = lax.broadcasted_iota(jnp.int32, (sources, ranks), 1)
    low = lane < half
    for f in range(freqs):
        v_copies[f].wait()
        for r in order:
            row = flipped(me, r)
            blocks = jnp.dot(data_ref[f], v_ref[f, row], preferred_element_type=jnp.float32)
            kept = lane < ranks_ref[f, row, me]
            real = jnp.where(kept, blocks[:sources], 0.0)
            imag = jnp.where(kept, blocks[sources:], 0.0)
            packed = jnp.where(low, real, pltpu.roll(imag, half, 1)).astype(jnp.bfloat16)
            if r == 0:
                recv_ref[f, me] = packed
                own_ref[f] = jnp.where(low, pltpu.roll(real, half, 1), imag).astype(jnp.bfloat16)
            else:
                send_ref[f, r] = packed
                if f == 0 and r == order[0]:
                    pl.semaphore_wait(barrier, tiles - 1 + parts - 1)
                space_copy(f, r).start()

    wide_lane = lax.broadcasted_iota(jnp.int32, (tile, ranks), 1)
    wide_low = wide_lane < half
    for f in range(freqs):
        u_copies[f].wait()
        for c in range(2):
            wide_ref[c] = u_ref[f, c].astype(jnp.float32)
        for j in range(tiles + 1):
            start = j if j < tiles else me
            real = wide_ref[0, pl.ds(start, tile, stride=tiles), :]
            imag = wide_ref[1, pl.ds(start, tile, stride=tiles), :]
            real_roll = pltpu.roll(real, half, 1)
            imag_roll = pltpu.roll(imag, half, 1)
            if j < tiles:
                top = jnp.where(wide_low, real, -imag_roll)
                bottom = jnp.where(wide_low, imag, real_roll)
            else:
                top = jnp.where(wide_low, real_roll, -imag)
                bottom = jnp.where(wide_low, imag_roll, real)
            factor_ref[f, j, :tile] = top.astype(jnp.bfloat16)
            factor_ref[f, j, tile:] = bottom.astype(jnp.bfloat16)

    for f in range(freqs):
        total = lax.dot_general(
            own_ref[f], factor_ref[f, tiles], NT_DIMS, preferred_element_type=jnp.float32
        )
        for r in range(1, tiles):
            space_copy(f, r).wait_recv()
        for j in range(0, tiles, 2):
            lhs = jnp.concatenate([recv_ref[f, j], recv_ref[f, j + 1]], axis=1)
            rhs = jnp.concatenate([factor_ref[f, j], factor_ref[f, j + 1]], axis=1)
            total += lax.dot_general(lhs, rhs, NT_DIMS, preferred_element_type=jnp.float32)
        spec_ref[f] = total.astype(jnp.bfloat16)
        for r in range(1, parts):
            freq_copy(f, r).start()
        out_ref[me_z, f] = spec_ref[f, pl.ds(pl.multiple_of(me_z * share, share), share), :]

    for f in range(freqs):
        for r in range(1, tiles):
            space_copy(f, r).wait_send()
        for r in range(1, parts):
            freq_copy(f, r).wait_send()
            freq_copy(f, r).wait_recv()


def time_kernel(tile, spec_ref, mute_ref, basis_hbm, out_hbm, lhs_ref, basis_ref, rows_ref, basis_sem, out_sems):
    parts, freqs, share, _ = spec_ref.shape
    chunk = 64
    groups = share // GROUP
    basis_copy = pltpu.make_async_copy(basis_hbm, basis_ref, basis_sem)
    basis_copy.start()
    mute = mute_ref[...].T
    for side in range(tile // 128):
        for g in range(groups):
            pieces = []
            for z in range(parts):
                for f in range(freqs):
                    for c in range(2):
                        at = c * tile + side * 128
                        piece = spec_ref[z, f, :, at : at + 128].astype(jnp.float32)
                        pieces.append(piece[g * GROUP : (g + 1) * GROUP])
            block = jnp.concatenate(pieces, axis=0)
            lhs_ref[g, side * 128 : (side + 1) * 128, :] = block.T.astype(jnp.bfloat16)
    basis_copy.wait()
    times = lax.broadcasted_iota(jnp.int32, (chunk, NT), 1)
    copies = []
    for n in range(tile // chunk):
        lhs = jnp.concatenate([lhs_ref[g, n * chunk : (n + 1) * chunk, :] for g in range(groups)], axis=0)
        lhs = jnp.concatenate([lhs, lhs], axis=1)
        for pair in range(GROUP // 2):
            product = jnp.dot(
                lhs, basis_ref[:, pair * 2 * NT : (pair + 1) * 2 * NT], preferred_element_type=jnp.float32
            )
            for g in range(groups):
                for e in range(2):
                    s = g * GROUP + pair * 2 + e
                    values = product[g * chunk : (g + 1) * chunk, e * NT : (e + 1) * NT]
                    starts = mute[n * chunk : (n + 1) * chunk, s : s + 1]
                    rows_ref[pl.ds(n * chunk * share + s, chunk, stride=share), :] = jnp.where(
                        times >= starts, values, 0.0
                    )
        span = pl.ds(n * chunk * share, chunk * share)
        copy = pltpu.make_async_copy(rows_ref.at[span], out_hbm.at[span], out_sems.at[n])
        copy.start()
        copies.append(copy)
    for copy in copies:
        copy.wait()


def block_basis(freq_total):
    weights = 1 + np.arange(freq_total) * (NT // 2 // freq_total)
    phase = (weights[:, None] * np.arange(NT)[None, :] % NT) * (2.0 * math.pi / NT)
    scale = 1.0 / math.sqrt(2.0 * freq_total)
    table = np.stack([np.cos(phase) * scale, -np.sin(phase) * scale], axis=1)
    table = table.reshape(2 * freq_total, NT).astype(np.float32)
    high = table.astype(ml_dtypes.bfloat16)
    low = (table - high.astype(np.float32)).astype(ml_dtypes.bfloat16)
    both = np.stack([high, low])
    full = np.zeros((2, 2 * freq_total, GROUP, GROUP, NT), ml_dtypes.bfloat16)
    for g in range(GROUP):
        full[:, :, g, g, :] = both
    return full.reshape(4 * freq_total * GROUP, GROUP * NT)


def shards(tiles, parts, basis, recorded, v_factors, u_factors, tile_ranks, mute_start):
    freqs, _, tile, sources = recorded.shape
    ranks = v_factors.shape[4]
    share = sources // parts
    bf16 = jnp.bfloat16
    spectra = pl.pallas_call(
        functools.partial(spectra_kernel, tiles, parts),
        out_shape=jax.ShapeDtypeStruct((parts, freqs, share, 2 * tile), bf16),
        in_specs=[
            pl.BlockSpec(memory_space=pltpu.SMEM),
            pl.BlockSpec(memory_space=pltpu.VMEM),
            pl.BlockSpec(memory_space=pl.ANY),
            pl.BlockSpec(memory_space=pl.ANY),
        ],
        out_specs=pl.BlockSpec(memory_space=pltpu.VMEM),
        scratch_shapes=[
            pltpu.VMEM((freqs, tiles, 2 * tile, ranks), bf16),
            pltpu.VMEM((freqs, 2, tile * tiles, ranks), bf16),
            pltpu.VMEM((2, tile * tiles, ranks), jnp.float32),
            pltpu.VMEM((freqs, 2 * sources, 2 * tile), bf16),
            pltpu.VMEM((freqs, tiles, sources, ranks), bf16),
            pltpu.VMEM((freqs, tiles, sources, ranks), bf16),
            pltpu.VMEM((freqs, sources, ranks), bf16),
            pltpu.VMEM((freqs, tiles + 1, 2 * tile, ranks), bf16),
            pltpu.VMEM((freqs, sources, 2 * tile), bf16),
            pltpu.SemaphoreType.DMA((freqs,)),
            pltpu.SemaphoreType.DMA((freqs,)),
            pltpu.SemaphoreType.DMA((freqs, tiles)),
            pltpu.SemaphoreType.DMA((freqs, tiles)),
            pltpu.SemaphoreType.DMA((freqs, parts)),
            pltpu.SemaphoreType.DMA((freqs, parts)),
        ],
        compiler_params=pltpu.CompilerParams(collective_id=0, has_side_effects=True),
        name="spectra_kernel",
    )(
        tile_ranks,
        recorded,
        v_factors.reshape(freqs, tiles, 2 * tile, ranks),
        u_factors.reshape(freqs, 2, tile * tiles, ranks),
    )
    traces = pl.pallas_call(
        functools.partial(time_kernel, tile),
        out_shape=jax.ShapeDtypeStruct((tile * share, NT), jnp.float32),
        in_specs=[
            pl.BlockSpec(memory_space=pltpu.VMEM),
            pl.BlockSpec(memory_space=pltpu.VMEM),
            pl.BlockSpec(memory_space=pl.ANY),
        ],
        out_specs=pl.BlockSpec(memory_space=pl.ANY),
        scratch_shapes=[
            pltpu.VMEM((share // GROUP, tile, 128), bf16),
            pltpu.VMEM(basis.shape, bf16),
            pltpu.VMEM((tile * share, NT), jnp.float32),
            pltpu.SemaphoreType.DMA,
            pltpu.SemaphoreType.DMA((tile // 64,)),
        ],
        name="time_kernel",
    )(spectra, mute_start.T, jnp.asarray(basis))
    return traces.reshape(tile, share, NT)


def solution(mesh):
    placed = (
        P("freq", None, "space", None),
        P("freq", None, None, "space", None),
        P("freq", None, "space", None, None),
        P("freq", None, None),
        P("space", "freq"),
    )
    tiles, parts = mesh.shape["space"], mesh.shape["freq"]

    def run(*args):
        body = functools.partial(shards, tiles, parts, block_basis(args[0].shape[0]))
        return jax.shard_map(
            body, mesh=mesh, in_specs=placed, out_specs=P("space", "freq", None), check_vma=False
        )(*args)

    return run
```

```python
import functools
import math

import jax
import jax.numpy as jnp
import ml_dtypes
import numpy as np
from jax import lax
from jax.experimental import pallas as pl
from jax.experimental.pallas import tpu as pltpu
from jax.sharding import PartitionSpec as P

NT = 128
GROUP = 8
NT_DIMS = (((1,), (1,)), ((), ()))


def flipped(index, mask):
    result = index
    bit = 1
    while bit <= mask:
        if mask & bit:
            result = result + bit * (1 - 2 * ((index // bit) % 2))
        bit *= 2
    return result


def send_order(count):
    return sorted(range(count), key=lambda r: (-bin(r >> 1).count("1"), r % 2, r))


def spectra_kernel(
    tiles, parts, ranks_ref, recorded_ref, v_hbm, u_hbm, out_ref,
    v_ref, u_ref, wide_ref, data_ref, send_ref, recv_ref, own_ref, factor_ref, spec_ref,
    v_sems, u_sems, send_sems, recv_sems, zsend_sems, zrecv_sems,
):
    me = lax.axis_index("space")
    me_z = lax.axis_index("freq")
    freqs = recorded_ref.shape[0]
    tile = recorded_ref.shape[2]
    sources = recorded_ref.shape[3]
    ranks = v_ref.shape[3]
    half = ranks // 2
    share = sources // parts
    order = send_order(tiles)

    v_copies = [
        pltpu.make_async_copy(v_hbm.at[f], v_ref.at[f], v_sems.at[f]) for f in range(freqs)
    ]
    u_copies = [
        pltpu.make_async_copy(u_hbm.at[f], u_ref.at[f], u_sems.at[f]) for f in range(freqs)
    ]
    for f in range(freqs):
        v_copies[f].start()
    for f in range(freqs):
        u_copies[f].start()

    barrier = pltpu.get_barrier_semaphore()
    for r in range(1, tiles):
        pl.semaphore_signal(
            barrier, inc=1, device_id={"space": flipped(me, r)}, device_id_type=pl.DeviceIdType.MESH
        )
    for r in range(1, parts):
        pl.semaphore_signal(
            barrier, inc=1, device_id={"freq": flipped(me_z, r)},
            device_id_type=pl.DeviceIdType.MESH,
        )

    def space_copy(f, r):
        return pltpu.make_async_remote_copy(
            src_ref=send_ref.at[f, r],
            dst_ref=recv_ref.at[f, me],
            send_sem=send_sems.at[f, r],
            recv_sem=recv_sems.at[f, r],
            device_id={"space": flipped(me, r)},
            device_id_type=pl.DeviceIdType.MESH,
        )

    def freq_copy(f, r):
        target = flipped(me_z, r)
        return pltpu.make_async_remote_copy(
            src_ref=spec_ref.at[f, target],
            dst_ref=out_ref.at[me_z, f],
            send_sem=zsend_sems.at[f, r],
            recv_sem=zrecv_sems.at[f, r],
            device_id={"freq": target},
            device_id_type=pl.DeviceIdType.MESH,
        )

    for f in range(freqs):
        real = recorded_ref[f, 0].astype(jnp.float32).T.astype(jnp.bfloat16)
        imag = recorded_ref[f, 1].astype(jnp.float32).T.astype(jnp.bfloat16)
        data_ref[f, :sources, :tile] = real
        data_ref[f, :sources, tile:] = -imag
        data_ref[f, sources:, :tile] = imag
        data_ref[f, sources:, tile:] = real

    lane = lax.broadcasted_iota(jnp.int32, (sources, ranks), 1)
    low = lane < half
    rank_of = lax.rem(lane, half)
    for f in range(freqs):
        v_copies[f].wait()
        for first in range(0, tiles, 4):
            group = order[first : first + 4]
            rows = [flipped(me, r) for r in group]
            packed_v = jnp.concatenate([v_ref[f, row, :, :half] for row in rows], axis=1)
            blocks = jnp.dot(data_ref[f], packed_v, preferred_element_type=jnp.float32)
            for n, (r, row) in enumerate(zip(group, rows)):
                columns = slice((n // 2) * ranks, (n // 2 + 1) * ranks)
                real, imag = blocks[:sources, columns], blocks[sources:, columns]
                if n % 2 == 0:
                    packed = jnp.where(low, real, pltpu.roll(imag, half, 1))
                else:
                    packed = jnp.where(low, pltpu.roll(real, half, 1), imag)
                packed = jnp.where(rank_of < ranks_ref[f, row, me], packed, 0.0).astype(jnp.bfloat16)
                if r == 0:
                    recv_ref[f, me] = packed
                else:
                    send_ref[f, r] = packed
                    if f == 0 and r == order[0]:
                        pl.semaphore_wait(barrier, tiles - 1 + parts - 1)
                    space_copy(f, r).start()
    for f in range(freqs):
        blocks = jnp.dot(data_ref[f], v_ref[f, me], preferred_element_type=jnp.float32)
        packed = jnp.where(low, pltpu.roll(blocks[:sources], half, 1), blocks[sources:])
        kept = rank_of + half < ranks_ref[f, me, me]
        own_ref[f] = jnp.where(kept, packed, 0.0).astype(jnp.bfloat16)

    wide_lane = lax.broadcasted_iota(jnp.int32, (tile, ranks), 1)
    wide_low = wide_lane < half
    for f in range(freqs):
        u_copies[f].wait()
        for c in range(2):
            wide_ref[c] = u_ref[f, c].astype(jnp.float32)
        for j in range(tiles + 1):
            start = j if j < tiles else me
            real = wide_ref[0, pl.ds(start, tile, stride=tiles), :]
            imag = wide_ref[1, pl.ds(start, tile, stride=tiles), :]
            real_roll = pltpu.roll(real, half, 1)
            imag_roll = pltpu.roll(imag, half, 1)
            if j < tiles:
                top = jnp.where(wide_low, real, -imag_roll)
                bottom = jnp.where(wide_low, imag, real_roll)
            else:
                top = jnp.where(wide_low, real_roll, -imag)
                bottom = jnp.where(wide_low, imag_roll, real)
            factor_ref[f, j, :tile] = top.astype(jnp.bfloat16)
            factor_ref[f, j, tile:] = bottom.astype(jnp.bfloat16)

    rows = tile // parts
    swap_lane = lax.broadcasted_iota(jnp.int32, (rows, sources), 1)
    for f in range(freqs):
        total = lax.dot_general(
            factor_ref[f, tiles], own_ref[f], NT_DIMS, preferred_element_type=jnp.float32
        )
        for r in range(1, tiles):
            space_copy(f, r).wait_recv()
        for j in range(0, tiles, 2):
            lhs = jnp.concatenate([factor_ref[f, j], factor_ref[f, j + 1]], axis=1)
            rhs = jnp.concatenate([recv_ref[f, j], recv_ref[f, j + 1]], axis=1)
            total += lax.dot_general(lhs, rhs, NT_DIMS, preferred_element_type=jnp.float32)
        for c in range(2):
            pieces = [total[c * tile + q * rows : c * tile + (q + 1) * rows] for q in range(parts)]
            bit = parts // 2
            while bit >= 1:
                width = bit * share
                keep = lax.rem(swap_lane, 2 * width) < width
                swapped = list(pieces)
                for q in range(parts):
                    if not q & bit:
                        x, y = pieces[q], pieces[q + bit]
                        swapped[q] = jnp.where(keep, x, pltpu.roll(y, width, 1))
                        swapped[q + bit] = jnp.where(keep, pltpu.roll(x, sources - width, 1), y)
                pieces = swapped
                bit //= 2
            for z in range(parts):
                spec_ref[f, z, c * rows : (c + 1) * rows] = pieces[z].astype(jnp.bfloat16)
        for r in range(parts - 1, 0, -1):
            freq_copy(f, r).start()
        out_ref[me_z, f] = spec_ref[f, me_z]

    for f in range(freqs):
        for r in range(1, tiles):
            space_copy(f, r).wait_send()
        for r in range(1, parts):
            freq_copy(f, r).wait_send()
            freq_copy(f, r).wait_recv()


def time_kernel(share, spec_ref, mute_ref, basis_hbm, out_hbm, basis_ref, rows_ref, basis_sem, out_sems):
    parts, freqs, rows, sources = spec_ref.shape
    rows //= 2
    basis_copy = pltpu.make_async_copy(basis_hbm, basis_ref, basis_sem)
    basis_copy.start()
    times = lax.broadcasted_iota(jnp.int32, (share, NT), 1)
    copies = []
    for n in range(rows // (2 * GROUP)):
        sides = []
        for g in (2 * n, 2 * n + 1):
            pieces = []
            for z in range(parts):
                for f in range(freqs):
                    for c in range(2):
                        at = c * rows + g * GROUP
                        pieces.append(spec_ref[z, f, at : at + GROUP].astype(jnp.float32))
            block = jnp.concatenate(pieces, axis=0)
            sides.append(block.T.astype(jnp.bfloat16))
        lhs = jnp.concatenate(sides, axis=0)
        lhs = jnp.concatenate([lhs, lhs], axis=1)
        if n == 0:
            basis_copy.wait()
        for pair in range(GROUP // 2):
            product = jnp.dot(
                lhs, basis_ref[:, pair * 2 * NT : (pair + 1) * 2 * NT], preferred_element_type=jnp.float32
            )
            for side in range(2):
                for q in range(parts):
                    for e in range(2):
                        p = q * rows + (2 * n + side) * GROUP + pair * 2 + e
                        at = side * sources + q * share
                        values = product[at : at + share, e * NT : (e + 1) * NT]
                        starts = mute_ref[:, p : p + 1]
                        rows_ref[p * share : (p + 1) * share, :] = jnp.where(times >= starts, values, 0.0)
        for q in range(parts):
            span = pl.ds((q * rows + 2 * n * GROUP) * share, 2 * GROUP * share)
            copy = pltpu.make_async_copy(rows_ref.at[span], out_hbm.at[span], out_sems.at[n, q])
            copy.start()
            copies.append(copy)
    for copy in copies:
        copy.wait()


def block_basis(freq_total):
    weights = 1 + np.arange(freq_total) * (NT // 2 // freq_total)
    phase = (weights[:, None] * np.arange(NT)[None, :] % NT) * (2.0 * math.pi / NT)
    scale = 1.0 / math.sqrt(2.0 * freq_total)
    table = np.stack([np.cos(phase) * scale, -np.sin(phase) * scale], axis=1)
    table = table.reshape(2 * freq_total, NT).astype(np.float32)
    high = table.astype(ml_dtypes.bfloat16)
    low = (table - high.astype(np.float32)).astype(ml_dtypes.bfloat16)
    both = np.stack([high, low])
    full = np.zeros((2, 2 * freq_total, GROUP, GROUP, NT), ml_dtypes.bfloat16)
    for g in range(GROUP):
        full[:, :, g, g, :] = both
    return full.reshape(4 * freq_total * GROUP, GROUP * NT)


def shards(tiles, parts, basis, recorded, v_factors, u_factors, tile_ranks, mute_start):
    freqs, _, tile, sources = recorded.shape
    ranks = v_factors.shape[4]
    share = sources // parts
    bf16 = jnp.bfloat16
    spectra = pl.pallas_call(
        functools.partial(spectra_kernel, tiles, parts),
        out_shape=jax.ShapeDtypeStruct((parts, freqs, 2 * tile // parts, sources), bf16),
        in_specs=[
            pl.BlockSpec(memory_space=pltpu.SMEM),
            pl.BlockSpec(memory_space=pltpu.VMEM),
            pl.BlockSpec(memory_space=pl.ANY),
            pl.BlockSpec(memory_space=pl.ANY),
        ],
        out_specs=pl.BlockSpec(memory_space=pltpu.VMEM),
        scratch_shapes=[
            pltpu.VMEM((freqs, tiles, 2 * tile, ranks), bf16),
            pltpu.VMEM((freqs, 2, tile * tiles, ranks), bf16),
            pltpu.VMEM((2, tile * tiles, ranks), jnp.float32),
            pltpu.VMEM((freqs, 2 * sources, 2 * tile), bf16),
            pltpu.VMEM((freqs, tiles, sources, ranks), bf16),
            pltpu.VMEM((freqs, tiles, sources, ranks), bf16),
            pltpu.VMEM((freqs, sources, ranks), bf16),
            pltpu.VMEM((freqs, tiles + 1, 2 * tile, ranks), bf16),
            pltpu.VMEM((freqs, parts, 2 * tile // parts, sources), bf16),
            pltpu.SemaphoreType.DMA((freqs,)),
            pltpu.SemaphoreType.DMA((freqs,)),
            pltpu.SemaphoreType.DMA((freqs, tiles)),
            pltpu.SemaphoreType.DMA((freqs, tiles)),
            pltpu.SemaphoreType.DMA((freqs, parts)),
            pltpu.SemaphoreType.DMA((freqs, parts)),
        ],
        compiler_params=pltpu.CompilerParams(collective_id=0, has_side_effects=True),
        name="spectra_kernel",
    )(
        tile_ranks,
        recorded,
        v_factors.reshape(freqs, tiles, 2 * tile, ranks),
        u_factors.reshape(freqs, 2, tile * tiles, ranks),
    )
    traces = pl.pallas_call(
        functools.partial(time_kernel, share),
        out_shape=jax.ShapeDtypeStruct((tile * share, NT), jnp.float32),
        in_specs=[
            pl.BlockSpec(memory_space=pltpu.VMEM),
            pl.BlockSpec(memory_space=pltpu.VMEM),
            pl.BlockSpec(memory_space=pl.ANY),
        ],
        out_specs=pl.BlockSpec(memory_space=pl.ANY),
        scratch_shapes=[
            pltpu.VMEM(basis.shape, bf16),
            pltpu.VMEM((tile * share, NT), jnp.float32),
            pltpu.SemaphoreType.DMA,
            pltpu.SemaphoreType.DMA((tile // parts // (2 * GROUP), parts)),
        ],
        name="time_kernel",
    )(spectra, mute_start.T, jnp.asarray(basis))
    return traces.reshape(tile, share, NT)


def solution(mesh):
    placed = (
        P("freq", None, "space", None),
        P("freq", None, None, "space", None),
        P("freq", None, "space", None, None),
        P("freq", None, None),
        P("space", "freq"),
    )
    tiles, parts = mesh.shape["space"], mesh.shape["freq"]

    def run(*args):
        body = functools.partial(shards, tiles, parts, block_basis(args[0].shape[0]))
        return jax.shard_map(
            body, mesh=mesh, in_specs=placed, out_specs=P("space", "freq", None), check_vma=False
        )(*args)

    return run
```

```python
import functools
import math

import jax
import jax.numpy as jnp
import ml_dtypes
import numpy as np
from jax import lax
from jax.experimental import pallas as pl
from jax.experimental.pallas import tpu as pltpu
from jax.sharding import PartitionSpec as P

NT = 128
GROUP = 8
NT_DIMS = (((1,), (1,)), ((), ()))


def flipped(index, mask):
    result = index
    bit = 1
    while bit <= mask:
        if mask & bit:
            result = result + bit * (1 - 2 * ((index // bit) % 2))
        bit *= 2
    return result


def send_order(count):
    return sorted(range(count), key=lambda r: (-bin(r >> 1).count("1"), r % 2, r))


def spectra_kernel(
    tiles, parts, ranks_hbm, recorded_hbm, v_hbm, u_hbm, mute_hbm, out_hbm, mask_hbm,
    ranks_ref, recorded_ref, mute_ref, mask_ref, v_ref, u_ref, wide_ref, data_ref, send_ref, recv_ref, own_ref, factor_ref, spec_ref,
    v_sems, u_sems, send_sems, recv_sems, zsend_sems, zrecv_sems,
    keep_sems, first_sems, mask_sems,
):
    me = lax.axis_index("space")
    me_z = lax.axis_index("freq")
    freqs = recorded_ref.shape[0]
    tile = recorded_ref.shape[2]
    sources = recorded_ref.shape[3]
    ranks = v_ref.shape[3]
    half = ranks // 2
    share = sources // parts
    order = send_order(tiles)

    v_copies = [
        pltpu.make_async_copy(v_hbm.at[f], v_ref.at[f], v_sems.at[f]) for f in range(freqs)
    ]
    u_copies = [
        pltpu.make_async_copy(u_hbm.at[f], u_ref.at[f], u_sems.at[f]) for f in range(freqs)
    ]
    ranks_copy = pltpu.make_async_copy(ranks_hbm, ranks_ref, first_sems.at[0])
    data_copy = pltpu.make_async_copy(recorded_hbm, recorded_ref, first_sems.at[1])
    mute_copy = pltpu.make_async_copy(mute_hbm, mute_ref, first_sems.at[2])
    data_copy.start()
    ranks_copy.start()
    for copy in v_copies + u_copies:
        copy.start()
    mute_copy.start()

    barrier = pltpu.get_barrier_semaphore()
    for r in range(1, tiles):
        pl.semaphore_signal(
            barrier, inc=1, device_id={"space": flipped(me, r)}, device_id_type=pl.DeviceIdType.MESH
        )
    for r in range(1, parts):
        pl.semaphore_signal(
            barrier, inc=1, device_id={"freq": flipped(me_z, r)},
            device_id_type=pl.DeviceIdType.MESH,
        )

    def space_copy(f, r):
        return pltpu.make_async_remote_copy(
            src_ref=send_ref.at[f, r],
            dst_ref=recv_ref.at[f, me],
            send_sem=send_sems.at[f, r],
            recv_sem=recv_sems.at[f, r],
            device_id={"space": flipped(me, r)},
            device_id_type=pl.DeviceIdType.MESH,
        )

    rows = tile // parts

    def freq_copy(f, c, r):
        target = flipped(me_z, r)
        return pltpu.make_async_remote_copy(
            src_ref=spec_ref.at[f, target, pl.ds(c * rows, rows)],
            dst_ref=out_hbm.at[me_z, f, pl.ds(c * rows, rows)],
            send_sem=zsend_sems.at[f, c, r],
            recv_sem=zrecv_sems.at[f, c, r],
            device_id={"freq": target},
            device_id_type=pl.DeviceIdType.MESH,
        )

    def keep_copy(f, c):
        return pltpu.make_async_copy(
            spec_ref.at[f, me_z, pl.ds(c * rows, rows)],
            out_hbm.at[me_z, f, pl.ds(c * rows, rows)],
            keep_sems.at[f, c],
        )

    data_copy.wait()
    for f in range(freqs):
        real = recorded_ref[f, 0].astype(jnp.float32).T.astype(jnp.bfloat16)
        imag = recorded_ref[f, 1].astype(jnp.float32).T.astype(jnp.bfloat16)
        data_ref[f, :sources, :tile] = real
        data_ref[f, :sources, tile:] = -imag
        data_ref[f, sources:, :tile] = imag
        data_ref[f, sources:, tile:] = real

    lane = lax.broadcasted_iota(jnp.int32, (sources, ranks), 1)
    low = lane < half
    rank_of = lax.rem(lane, half)
    ranks_copy.wait()
    for f in range(freqs):
        v_copies[f].wait()
        for first in range(0, tiles, 4):
            group = order[first : first + 4]
            targets = [flipped(me, r) for r in group]
            packed_v = jnp.concatenate([v_ref[f, row, :, :half] for row in targets], axis=1)
            blocks = jnp.dot(data_ref[f], packed_v, preferred_element_type=jnp.float32)
            for n, (r, row) in enumerate(zip(group, targets)):
                columns = slice((n // 2) * ranks, (n // 2 + 1) * ranks)
                real, imag = blocks[:sources, columns], blocks[sources:, columns]
                if n % 2 == 0:
                    packed = jnp.where(low, real, pltpu.roll(imag, half, 1))
                else:
                    packed = jnp.where(low, pltpu.roll(real, half, 1), imag)
                packed = jnp.where(rank_of < ranks_ref[f, row, me], packed, 0.0).astype(jnp.bfloat16)
                if r == 0:
                    recv_ref[f, me] = packed
                else:
                    send_ref[f, r] = packed
                    if f == 0 and r == order[0]:
                        pl.semaphore_wait(barrier, tiles - 1 + parts - 1)
                    space_copy(f, r).start()
    for f in range(freqs):
        blocks = jnp.dot(data_ref[f], v_ref[f, me], preferred_element_type=jnp.float32)
        packed = jnp.where(low, pltpu.roll(blocks[:sources], half, 1), blocks[sources:])
        kept = rank_of + half < ranks_ref[f, me, me]
        own_ref[f] = jnp.where(kept, packed, 0.0).astype(jnp.bfloat16)

    wide_lane = lax.broadcasted_iota(jnp.int32, (tile, ranks), 1)
    wide_low = wide_lane < half
    for f in range(freqs):
        u_copies[f].wait()
        for c in range(2):
            wide_ref[c] = u_ref[f, c].astype(jnp.float32)
        for j in range(tiles + 1):
            start = j if j < tiles else me
            real = wide_ref[0, pl.ds(start, tile, stride=tiles), :]
            imag = wide_ref[1, pl.ds(start, tile, stride=tiles), :]
            real_roll = pltpu.roll(real, half, 1)
            imag_roll = pltpu.roll(imag, half, 1)
            if j < tiles:
                top = jnp.where(wide_low, real, -imag_roll)
                bottom = jnp.where(wide_low, imag, real_roll)
            else:
                top = jnp.where(wide_low, real_roll, -imag)
                bottom = jnp.where(wide_low, imag_roll, real)
            factor_ref[f, j, :tile] = top.astype(jnp.bfloat16)
            factor_ref[f, j, tile:] = bottom.astype(jnp.bfloat16)

    swap_lane = lax.broadcasted_iota(jnp.int32, (rows, sources), 1)
    for f in range(freqs):
        total = lax.dot_general(
            factor_ref[f, tiles], own_ref[f], NT_DIMS, preferred_element_type=jnp.float32
        )
        for first in [0] + list(range(2, tiles, 2))[::-1]:
            pair = [flipped(me, first), flipped(me, first + 1)]
            for r in (first, first + 1):
                if r > 0:
                    space_copy(f, r).wait_recv()
            lhs = jnp.concatenate([factor_ref[f, j] for j in pair], axis=1)
            rhs = jnp.concatenate([recv_ref[f, j] for j in pair], axis=1)
            total += lax.dot_general(lhs, rhs, NT_DIMS, preferred_element_type=jnp.float32)
        for c in range(2):
            pieces = [total[c * tile + q * rows : c * tile + (q + 1) * rows] for q in range(parts)]
            bit = parts // 2
            while bit >= 1:
                width = bit * share
                keep = lax.rem(swap_lane, 2 * width) < width
                swapped = list(pieces)
                for q in range(parts):
                    if not q & bit:
                        x, y = pieces[q], pieces[q + bit]
                        swapped[q] = jnp.where(keep, x, pltpu.roll(y, width, 1))
                        swapped[q + bit] = jnp.where(keep, pltpu.roll(x, sources - width, 1), y)
                pieces = swapped
                bit //= 2
            for z in range(parts):
                spec_ref[f, z, c * rows : (c + 1) * rows] = pieces[z].astype(jnp.bfloat16)
            for r in range(parts - 1, 0, -1):
                freq_copy(f, c, r).start()
            keep_copy(f, c).start()

    mute_copy.wait()
    times = lax.broadcasted_iota(jnp.int32, (share, NT), 1)
    span = 2 * GROUP
    mask_copies = []
    for n in range(rows // span):
        for q in range(parts):
            for i in range(span):
                p = q * rows + n * span + i
                at = (q * span + i) * share
                starts = mute_ref[:, p : p + 1]
                mask_ref[n, at : at + share] = jnp.where(times >= starts, 1.0, 0.0).astype(jnp.bfloat16)
        copy = pltpu.make_async_copy(mask_ref.at[n], mask_hbm.at[n], mask_sems.at[n])
        copy.start()
        mask_copies.append(copy)

    for copy in mask_copies:
        copy.wait()
    for f in range(freqs):
        for r in range(1, tiles):
            space_copy(f, r).wait_send()
        for c in range(2):
            keep_copy(f, c).wait()
            for r in range(1, parts):
                freq_copy(f, c, r).wait_send()
                freq_copy(f, c, r).wait_recv()


def time_kernel(
    share, spec_hbm, mask_hbm, basis_hbm, out_hbm,
    spec_ref, mask_ref, basis_ref, rows_ref, in_sems, mask_sems, out_sems,
):
    parts, freqs, rows, sources = spec_ref.shape
    rows //= 2
    spec_copy = pltpu.make_async_copy(spec_hbm, spec_ref, in_sems.at[0])
    spec_copy.start()
    basis_copy = pltpu.make_async_copy(basis_hbm, basis_ref, in_sems.at[1])
    basis_copy.start()
    mask_copies = [
        pltpu.make_async_copy(mask_hbm.at[n], mask_ref.at[n], mask_sems.at[n])
        for n in range(mask_ref.shape[0])
    ]
    for copy in mask_copies:
        copy.start()
    spec_copy.wait()
    copies = []
    for n in range(rows // (2 * GROUP)):
        sides = []
        for g in (2 * n, 2 * n + 1):
            pieces = []
            for z in range(parts):
                for f in range(freqs):
                    for c in range(2):
                        at = c * rows + g * GROUP
                        pieces.append(spec_ref[z, f, at : at + GROUP].astype(jnp.float32))
            block = jnp.concatenate(pieces, axis=0)
            sides.append(block.T.astype(jnp.bfloat16))
        lhs = jnp.concatenate(sides, axis=0)
        lhs = jnp.concatenate([lhs, lhs], axis=1)
        if n == 0:
            basis_copy.wait()
        mask_copies[n].wait()
        for pair in range(GROUP // 2):
            product = jnp.dot(
                lhs, basis_ref[:, pair * 2 * NT : (pair + 1) * 2 * NT], preferred_element_type=jnp.float32
            )
            for side in range(2):
                for q in range(parts):
                    for e in range(2):
                        p = q * rows + (2 * n + side) * GROUP + pair * 2 + e
                        at = side * sources + q * share
                        values = product[at : at + share, e * NT : (e + 1) * NT]
                        row = (q * 2 * GROUP + side * GROUP + pair * 2 + e) * share
                        mask = mask_ref[n, row : row + share].astype(jnp.float32)
                        rows_ref[p * share : (p + 1) * share, :] = values * mask
        for q in range(parts):
            span = pl.ds((q * rows + 2 * n * GROUP) * share, 2 * GROUP * share)
            copy = pltpu.make_async_copy(rows_ref.at[span], out_hbm.at[span], out_sems.at[n, q])
            copy.start()
            copies.append(copy)
    for copy in copies:
        copy.wait()


def block_basis(freq_total):
    weights = 1 + np.arange(freq_total) * (NT // 2 // freq_total)
    phase = (weights[:, None] * np.arange(NT)[None, :] % NT) * (2.0 * math.pi / NT)
    scale = 1.0 / math.sqrt(2.0 * freq_total)
    table = np.stack([np.cos(phase) * scale, -np.sin(phase) * scale], axis=1)
    table = table.reshape(2 * freq_total, NT).astype(np.float32)
    high = table.astype(ml_dtypes.bfloat16)
    low = (table - high.astype(np.float32)).astype(ml_dtypes.bfloat16)
    both = np.stack([high, low])
    full = np.zeros((2, 2 * freq_total, GROUP, GROUP, NT), ml_dtypes.bfloat16)
    for g in range(GROUP):
        full[:, :, g, g, :] = both
    return full.reshape(4 * freq_total * GROUP, GROUP * NT)


def shards(tiles, parts, basis, recorded, v_factors, u_factors, tile_ranks, mute_start):
    freqs, _, tile, sources = recorded.shape
    ranks = v_factors.shape[4]
    share = sources // parts
    bf16 = jnp.bfloat16
    spec_shape = (parts, freqs, 2 * tile // parts, sources)
    chunks = tile // parts // (2 * GROUP)
    mask_shape = (chunks, tile * share // chunks, NT)
    anywhere = pl.BlockSpec(memory_space=pl.ANY)
    spectra, mask = pl.pallas_call(
        functools.partial(spectra_kernel, tiles, parts),
        out_shape=(jax.ShapeDtypeStruct(spec_shape, bf16), jax.ShapeDtypeStruct(mask_shape, bf16)),
        in_specs=[anywhere] * 5,
        out_specs=(anywhere, anywhere),
        scratch_shapes=[
            pltpu.SMEM(tile_ranks.shape, jnp.int32),
            pltpu.VMEM(recorded.shape, bf16),
            pltpu.VMEM((share, tile), jnp.int32),
            pltpu.VMEM(mask_shape, bf16),
            pltpu.VMEM((freqs, tiles, 2 * tile, ranks), bf16),
            pltpu.VMEM((freqs, 2, tile * tiles, ranks), bf16),
            pltpu.VMEM((2, tile * tiles, ranks), jnp.float32),
            pltpu.VMEM((freqs, 2 * sources, 2 * tile), bf16),
            pltpu.VMEM((freqs, tiles, sources, ranks), bf16),
            pltpu.VMEM((freqs, tiles, sources, ranks), bf16),
            pltpu.VMEM((freqs, sources, ranks), bf16),
            pltpu.VMEM((freqs, tiles + 1, 2 * tile, ranks), bf16),
            pltpu.VMEM((freqs, parts, 2 * tile // parts, sources), bf16),
            pltpu.SemaphoreType.DMA((freqs,)),
            pltpu.SemaphoreType.DMA((freqs,)),
            pltpu.SemaphoreType.DMA((freqs, tiles)),
            pltpu.SemaphoreType.DMA((freqs, tiles)),
            pltpu.SemaphoreType.DMA((freqs, 2, parts)),
            pltpu.SemaphoreType.DMA((freqs, 2, parts)),
            pltpu.SemaphoreType.DMA((freqs, 2)),
            pltpu.SemaphoreType.DMA((3,)),
            pltpu.SemaphoreType.DMA((chunks,)),
        ],
        compiler_params=pltpu.CompilerParams(collective_id=0, has_side_effects=True),
        name="spectra_kernel",
    )(
        tile_ranks,
        recorded,
        v_factors.reshape(freqs, tiles, 2 * tile, ranks),
        u_factors.reshape(freqs, 2, tile * tiles, ranks),
        mute_start.T,
    )
    traces = pl.pallas_call(
        functools.partial(time_kernel, share),
        out_shape=jax.ShapeDtypeStruct((tile * share, NT), jnp.float32),
        in_specs=[anywhere] * 3,
        out_specs=anywhere,
        scratch_shapes=[
            pltpu.VMEM(spec_shape, bf16),
            pltpu.VMEM(mask_shape, bf16),
            pltpu.VMEM(basis.shape, bf16),
            pltpu.VMEM((tile * share, NT), jnp.float32),
            pltpu.SemaphoreType.DMA((2,)),
            pltpu.SemaphoreType.DMA((chunks,)),
            pltpu.SemaphoreType.DMA((chunks, parts)),
        ],
        name="time_kernel",
    )(spectra, mask, jnp.asarray(basis))
    return traces.reshape(tile, share, NT)


def solution(mesh):
    placed = (
        P("freq", None, "space", None),
        P("freq", None, None, "space", None),
        P("freq", None, "space", None, None),
        P("freq", None, None),
        P("space", "freq"),
    )
    tiles, parts = mesh.shape["space"], mesh.shape["freq"]

    def run(*args):
        body = functools.partial(shards, tiles, parts, block_basis(args[0].shape[0]))
        return jax.shard_map(
            body, mesh=mesh, in_specs=placed, out_specs=P("space", "freq", None), check_vma=False
        )(*args)

    return run
```

```python
import functools
import math

import jax
import jax.numpy as jnp
import ml_dtypes
import numpy as np
from jax import lax
from jax.experimental import pallas as pl
from jax.experimental.pallas import tpu as pltpu
from jax.sharding import PartitionSpec as P

NT = 128
GROUP = 8
NT_DIMS = (((1,), (1,)), ((), ()))


def flipped(index, mask):
    result = index
    bit = 1
    while bit <= mask:
        if mask & bit:
            result = result + bit * (1 - 2 * ((index // bit) % 2))
        bit *= 2
    return result


def send_order(count):
    return sorted(range(count), key=lambda r: (-bin(r >> 1).count("1"), r % 2, r))


def spectra_kernel(
    tiles, parts, ranks_hbm, recorded_hbm, v_hbm, u_hbm, mute_hbm, out_hbm, mask_hbm,
    ranks_ref, recorded_ref, mute_ref, mask_ref, v_ref, u_ref, wide_ref, data_ref, send_ref, recv_ref, own_ref, factor_ref, spec_ref,
    v_sems, u_sems, send_sems, recv_sems, zsend_sems, zrecv_sems,
    keep_sems, first_sems, mask_sems,
):
    me = lax.axis_index("space")
    me_z = lax.axis_index("freq")
    freqs = recorded_ref.shape[0]
    tile = recorded_ref.shape[2]
    sources = recorded_ref.shape[3]
    ranks = v_ref.shape[3]
    half = ranks // 2
    share = sources // parts
    order = send_order(tiles)

    v_copies = [
        pltpu.make_async_copy(v_hbm.at[f], v_ref.at[f], v_sems.at[f]) for f in range(freqs)
    ]
    u_copies = [
        pltpu.make_async_copy(u_hbm.at[f], u_ref.at[f], u_sems.at[f]) for f in range(freqs)
    ]
    ranks_copy = pltpu.make_async_copy(ranks_hbm, ranks_ref, first_sems.at[0])
    data_copy = pltpu.make_async_copy(recorded_hbm, recorded_ref, first_sems.at[1])
    mute_copy = pltpu.make_async_copy(mute_hbm, mute_ref, first_sems.at[2])
    data_copy.start()
    ranks_copy.start()
    for copy in v_copies + u_copies:
        copy.start()
    mute_copy.start()

    barrier = pltpu.get_barrier_semaphore()
    for r in range(1, tiles):
        pl.semaphore_signal(
            barrier, inc=1, device_id={"space": flipped(me, r)}, device_id_type=pl.DeviceIdType.MESH
        )
    for r in range(1, parts):
        pl.semaphore_signal(
            barrier, inc=1, device_id={"freq": flipped(me_z, r)},
            device_id_type=pl.DeviceIdType.MESH,
        )

    def space_copy(f, r):
        return pltpu.make_async_remote_copy(
            src_ref=send_ref.at[f, r],
            dst_ref=recv_ref.at[f, me],
            send_sem=send_sems.at[f, r],
            recv_sem=recv_sems.at[f, r],
            device_id={"space": flipped(me, r)},
            device_id_type=pl.DeviceIdType.MESH,
        )

    rows = tile // parts

    def freq_copy(f, c, r):
        target = flipped(me_z, r)
        return pltpu.make_async_remote_copy(
            src_ref=spec_ref.at[f, target, pl.ds(c * rows, rows)],
            dst_ref=out_hbm.at[me_z, f, pl.ds(c * rows, rows)],
            send_sem=zsend_sems.at[f, c, r],
            recv_sem=zrecv_sems.at[f, c, r],
            device_id={"freq": target},
            device_id_type=pl.DeviceIdType.MESH,
        )

    def keep_copy(f, c):
        return pltpu.make_async_copy(
            spec_ref.at[f, me_z, pl.ds(c * rows, rows)],
            out_hbm.at[me_z, f, pl.ds(c * rows, rows)],
            keep_sems.at[f, c],
        )

    data_copy.wait()
    lane = lax.broadcasted_iota(jnp.int32, (sources, ranks), 1)
    low = lane < half
    rank_of = lax.rem(lane, half)
    ranks_copy.wait()
    for f in range(freqs):
        real = recorded_ref[f, 0].astype(jnp.float32).T.astype(jnp.bfloat16)
        imag = recorded_ref[f, 1].astype(jnp.float32).T.astype(jnp.bfloat16)
        data_ref[f, :sources, :tile] = real
        data_ref[f, :sources, tile:] = -imag
        data_ref[f, sources:, :tile] = imag
        data_ref[f, sources:, tile:] = real
        v_copies[f].wait()
        for first in range(0, tiles, 4):
            group = order[first : first + 4]
            targets = [flipped(me, r) for r in group]
            packed_v = jnp.concatenate([v_ref[f, row, :, :half] for row in targets], axis=1)
            blocks = jnp.dot(data_ref[f], packed_v, preferred_element_type=jnp.float32)
            for n, (r, row) in enumerate(zip(group, targets)):
                columns = slice((n // 2) * ranks, (n // 2 + 1) * ranks)
                real, imag = blocks[:sources, columns], blocks[sources:, columns]
                if n % 2 == 0:
                    packed = jnp.where(low, real, pltpu.roll(imag, half, 1))
                else:
                    packed = jnp.where(low, pltpu.roll(real, half, 1), imag)
                packed = jnp.where(rank_of < ranks_ref[f, row, me], packed, 0.0).astype(jnp.bfloat16)
                if r == 0:
                    recv_ref[f, me] = packed
                else:
                    send_ref[f, r] = packed
                    if f == 0 and r == order[0]:
                        pl.semaphore_wait(barrier, tiles - 1 + parts - 1)
                    space_copy(f, r).start()
    for f in range(freqs):
        blocks = jnp.dot(data_ref[f], v_ref[f, me], preferred_element_type=jnp.float32)
        packed = jnp.where(low, pltpu.roll(blocks[:sources], half, 1), blocks[sources:])
        kept = rank_of + half < ranks_ref[f, me, me]
        own_ref[f] = jnp.where(kept, packed, 0.0).astype(jnp.bfloat16)

    wide_lane = lax.broadcasted_iota(jnp.int32, (tile, ranks), 1)
    wide_low = wide_lane < half
    def prepare(f):
        u_copies[f].wait()
        for c in range(2):
            wide_ref[c] = u_ref[f, c].astype(jnp.float32)
        for j in range(tiles + 1):
            start = j if j < tiles else me
            real = wide_ref[0, pl.ds(start, tile, stride=tiles), :]
            imag = wide_ref[1, pl.ds(start, tile, stride=tiles), :]
            real_roll = pltpu.roll(real, half, 1)
            imag_roll = pltpu.roll(imag, half, 1)
            if j < tiles:
                top = jnp.where(wide_low, real, -imag_roll)
                bottom = jnp.where(wide_low, imag, real_roll)
            else:
                top = jnp.where(wide_low, real_roll, -imag)
                bottom = jnp.where(wide_low, imag_roll, real)
            factor_ref[f, j, :tile] = top.astype(jnp.bfloat16)
            factor_ref[f, j, tile:] = bottom.astype(jnp.bfloat16)

    swap_lane = lax.broadcasted_iota(jnp.int32, (rows, sources), 1)
    for f in range(freqs):
        prepare(f)
        total = lax.dot_general(
            factor_ref[f, tiles], own_ref[f], NT_DIMS, preferred_element_type=jnp.float32
        )
        for first in [0] + list(range(2, tiles, 2))[::-1]:
            pair = [flipped(me, first), flipped(me, first + 1)]
            for r in (first, first + 1):
                if r > 0:
                    space_copy(f, r).wait_recv()
            lhs = jnp.concatenate([factor_ref[f, j] for j in pair], axis=1)
            rhs = jnp.concatenate([recv_ref[f, j] for j in pair], axis=1)
            total += lax.dot_general(lhs, rhs, NT_DIMS, preferred_element_type=jnp.float32)
        for c in range(2):
            pieces = [total[c * tile + q * rows : c * tile + (q + 1) * rows] for q in range(parts)]
            bit = parts // 2
            while bit >= 1:
                width = bit * share
                keep = lax.rem(swap_lane, 2 * width) < width
                swapped = list(pieces)
                for q in range(parts):
                    if not q & bit:
                        x, y = pieces[q], pieces[q + bit]
                        swapped[q] = jnp.where(keep, x, pltpu.roll(y, width, 1))
                        swapped[q + bit] = jnp.where(keep, pltpu.roll(x, sources - width, 1), y)
                pieces = swapped
                bit //= 2
            for z in range(parts):
                spec_ref[f, z, c * rows : (c + 1) * rows] = pieces[z].astype(jnp.bfloat16)
            for r in range(parts - 1, 0, -1):
                freq_copy(f, c, r).start()
            keep_copy(f, c).start()

    mute_copy.wait()
    times = lax.broadcasted_iota(jnp.int32, (share, NT), 1)
    span = 2 * GROUP
    mask_copies = []
    for n in range(rows // span):
        for q in range(parts):
            for i in range(span):
                p = q * rows + n * span + i
                at = (q * span + i) * share
                starts = mute_ref[:, p : p + 1]
                mask_ref[n, at : at + share] = jnp.where(times >= starts, 1.0, 0.0).astype(jnp.bfloat16)
        copy = pltpu.make_async_copy(mask_ref.at[n], mask_hbm.at[n], mask_sems.at[n])
        copy.start()
        mask_copies.append(copy)

    for copy in mask_copies:
        copy.wait()
    for f in range(freqs):
        for r in range(1, tiles):
            space_copy(f, r).wait_send()
        for c in range(2):
            keep_copy(f, c).wait()
            for r in range(1, parts):
                freq_copy(f, c, r).wait_send()
                freq_copy(f, c, r).wait_recv()


def time_kernel(
    share, spec_hbm, mask_hbm, basis_hbm, out_hbm,
    spec_ref, mask_ref, basis_ref, rows_ref, in_sems, mask_sems, out_sems,
):
    parts, freqs, rows, sources = spec_ref.shape
    rows //= 2
    spec_copy = pltpu.make_async_copy(spec_hbm, spec_ref, in_sems.at[0])
    spec_copy.start()
    basis_copy = pltpu.make_async_copy(basis_hbm, basis_ref, in_sems.at[1])
    basis_copy.start()
    mask_copies = [
        pltpu.make_async_copy(mask_hbm.at[n], mask_ref.at[n], mask_sems.at[n])
        for n in range(mask_ref.shape[0])
    ]
    for copy in mask_copies:
        copy.start()
    spec_copy.wait()
    copies = []
    for n in range(rows // (2 * GROUP)):
        sides = []
        for g in (2 * n, 2 * n + 1):
            pieces = []
            for z in range(parts):
                for f in range(freqs):
                    for c in range(2):
                        at = c * rows + g * GROUP
                        pieces.append(spec_ref[z, f, at : at + GROUP].astype(jnp.float32))
            block = jnp.concatenate(pieces, axis=0)
            sides.append(block.T.astype(jnp.bfloat16))
        lhs = jnp.concatenate(sides, axis=0)
        lhs = jnp.concatenate([lhs, lhs], axis=1)
        if n == 0:
            basis_copy.wait()
        mask_copies[n].wait()
        for pair in range(GROUP // 2):
            product = jnp.dot(
                lhs, basis_ref[:, pair * 2 * NT : (pair + 1) * 2 * NT], preferred_element_type=jnp.float32
            )
            for side in range(2):
                for q in range(parts):
                    for e in range(2):
                        p = q * rows + (2 * n + side) * GROUP + pair * 2 + e
                        at = side * sources + q * share
                        values = product[at : at + share, e * NT : (e + 1) * NT]
                        row = (q * 2 * GROUP + side * GROUP + pair * 2 + e) * share
                        mask = mask_ref[n, row : row + share].astype(jnp.float32)
                        rows_ref[p * share : (p + 1) * share, :] = values * mask
        for q in range(parts):
            span = pl.ds((q * rows + 2 * n * GROUP) * share, 2 * GROUP * share)
            copy = pltpu.make_async_copy(rows_ref.at[span], out_hbm.at[span], out_sems.at[n, q])
            copy.start()
            copies.append(copy)
    for copy in copies:
        copy.wait()


def block_basis(freq_total):
    weights = 1 + np.arange(freq_total) * (NT // 2 // freq_total)
    phase = (weights[:, None] * np.arange(NT)[None, :] % NT) * (2.0 * math.pi / NT)
    scale = 1.0 / math.sqrt(2.0 * freq_total)
    table = np.stack([np.cos(phase) * scale, -np.sin(phase) * scale], axis=1)
    table = table.reshape(2 * freq_total, NT).astype(np.float32)
    high = table.astype(ml_dtypes.bfloat16)
    low = (table - high.astype(np.float32)).astype(ml_dtypes.bfloat16)
    both = np.stack([high, low])
    full = np.zeros((2, 2 * freq_total, GROUP, GROUP, NT), ml_dtypes.bfloat16)
    for g in range(GROUP):
        full[:, :, g, g, :] = both
    return full.reshape(4 * freq_total * GROUP, GROUP * NT)


def shards(tiles, parts, basis, recorded, v_factors, u_factors, tile_ranks, mute_start):
    freqs, _, tile, sources = recorded.shape
    ranks = v_factors.shape[4]
    share = sources // parts
    bf16 = jnp.bfloat16
    spec_shape = (parts, freqs, 2 * tile // parts, sources)
    chunks = tile // parts // (2 * GROUP)
    mask_shape = (chunks, tile * share // chunks, NT)
    anywhere = pl.BlockSpec(memory_space=pl.ANY)
    spectra, mask = pl.pallas_call(
        functools.partial(spectra_kernel, tiles, parts),
        out_shape=(jax.ShapeDtypeStruct(spec_shape, bf16), jax.ShapeDtypeStruct(mask_shape, bf16)),
        in_specs=[anywhere] * 5,
        out_specs=(anywhere, anywhere),
        scratch_shapes=[
            pltpu.SMEM(tile_ranks.shape, jnp.int32),
            pltpu.VMEM(recorded.shape, bf16),
            pltpu.VMEM((share, tile), jnp.int32),
            pltpu.VMEM(mask_shape, bf16),
            pltpu.VMEM((freqs, tiles, 2 * tile, ranks), bf16),
            pltpu.VMEM((freqs, 2, tile * tiles, ranks), bf16),
            pltpu.VMEM((2, tile * tiles, ranks), jnp.float32),
            pltpu.VMEM((freqs, 2 * sources, 2 * tile), bf16),
            pltpu.VMEM((freqs, tiles, sources, ranks), bf16),
            pltpu.VMEM((freqs, tiles, sources, ranks), bf16),
            pltpu.VMEM((freqs, sources, ranks), bf16),
            pltpu.VMEM((freqs, tiles + 1, 2 * tile, ranks), bf16),
            pltpu.VMEM((freqs, parts, 2 * tile // parts, sources), bf16),
            pltpu.SemaphoreType.DMA((freqs,)),
            pltpu.SemaphoreType.DMA((freqs,)),
            pltpu.SemaphoreType.DMA((freqs, tiles)),
            pltpu.SemaphoreType.DMA((freqs, tiles)),
            pltpu.SemaphoreType.DMA((freqs, 2, parts)),
            pltpu.SemaphoreType.DMA((freqs, 2, parts)),
            pltpu.SemaphoreType.DMA((freqs, 2)),
            pltpu.SemaphoreType.DMA((3,)),
            pltpu.SemaphoreType.DMA((chunks,)),
        ],
        compiler_params=pltpu.CompilerParams(collective_id=0, has_side_effects=True),
        name="spectra_kernel",
    )(
        tile_ranks,
        recorded,
        v_factors.reshape(freqs, tiles, 2 * tile, ranks),
        u_factors.reshape(freqs, 2, tile * tiles, ranks),
        mute_start.T,
    )
    traces = pl.pallas_call(
        functools.partial(time_kernel, share),
        out_shape=jax.ShapeDtypeStruct((tile * share, NT), jnp.float32),
        in_specs=[anywhere] * 3,
        out_specs=anywhere,
        scratch_shapes=[
            pltpu.VMEM(spec_shape, bf16),
            pltpu.VMEM(mask_shape, bf16),
            pltpu.VMEM(basis.shape, bf16),
            pltpu.VMEM((tile * share, NT), jnp.float32),
            pltpu.SemaphoreType.DMA((2,)),
            pltpu.SemaphoreType.DMA((chunks,)),
            pltpu.SemaphoreType.DMA((chunks, parts)),
        ],
        name="time_kernel",
    )(spectra, mask, jnp.asarray(basis))
    return traces.reshape(tile, share, NT)


def solution(mesh):
    placed = (
        P("freq", None, "space", None),
        P("freq", None, None, "space", None),
        P("freq", None, "space", None, None),
        P("freq", None, None),
        P("space", "freq"),
    )
    tiles, parts = mesh.shape["space"], mesh.shape["freq"]

    def run(*args):
        body = functools.partial(shards, tiles, parts, block_basis(args[0].shape[0]))
        return jax.shard_map(
            body, mesh=mesh, in_specs=placed, out_specs=P("space", "freq", None), check_vma=False
        )(*args)

    return run
```
